128 devices in a mesh: row: 8 (over x, core), col: 16 (over y, z).
Axes of the slice: x: 4, y: 4, z: 4, core: 2. Of those that a mesh axis runs over, the one named last changes fastest.
Arguments:
- children: bfloat16 [20480, 10240], P('row', 'col'), may hold values from -6 to 6
- row_maps: int32 [2, 80], replicated, may hold values from 0 to 159, as said below
- col_maps: int32 [2, 80], replicated, may hold values from 0 to 159, as said below
- pairs: int32 [8192, 2], replicated, may hold values from 0 to 159, as said below
- lower_panel: bfloat16 [20480, 1024], P('row', 'col'), may hold values from -6 to 6
- upper_panel: bfloat16 [1024, 20480], P('row', 'col'), may hold values from -0.1875 to 0.1875
Outputs:
- front: float32 [20480, 20480], P('row', 'col')
The draws below stay inside these ranges and needn't reach their ends.
Inputs may be any that keep to these rules, and one draw needn't show every extreme that they name: Parent tile row r of the front's order is stored at tile row (r % 8) * 20 + r // 8. In the front's order each row of row_maps is increasing, child tile row i going to parent tile row 2 * i or 2 * i + 1. Of the 20 child tile rows b * 20 to b * 20 + 19 of one child, at most 5 map into any one stored block of tile rows a * 20 to a * 20 + 19, and in every such group of rows some block receives 5. Parent tile column r of the front's order is stored at tile column (r % 16) * 10 + r // 16. In the front's order each row of col_maps is increasing, child tile column j going to parent tile column 2 * j or 2 * j + 1. Of the 5 child tile columns b * 5 to b * 5 + 4 of one child, at most 1 map into any one stored block of tile columns a * 10 to a * 10 + 9, and in every such group some block receives 1. `pairs`: no pair is listed twice.
All inputs are finite; a program needn't handle non-finite values.
Results may differ from the reference program's by a relative error of at most 0.0003.
Values may be sent and summed in bfloat16 or wider, within the bound.
No kernel may reach another device: no remote copies, remote signals or barrier semaphores. Data moves between devices by JAX's collectives and lax.ppermute only.
A program may use at most 192 MiB of HBM per device.

```python
import jax
import jax.numpy as jnp
from jax import lax

TILE = 128
C = 10240
K = 1024
P_SIZE = 20480
CT = 80
PT = 160
KC = 5
CRB = 20
PRB = 20
PC = 10
NPAIRS = 8192
N_ROW = 8
N_COL = 16


def cyclic_law(key, per_block, classes, devices, per_device):
    tile_ids = jnp.arange(CT, dtype=jnp.int32)
    block = tile_ids // per_block
    within = tile_ids % per_block
    bits = jax.random.randint(jax.random.fold_in(key, 1), (CT,), 0, 2, dtype=jnp.int32)
    common = jax.random.randint(jax.random.fold_in(key, 2), (CT,), 0, 2, dtype=jnp.int32)
    chosen = jnp.where(within % classes == 0, common[block], bits)
    logical = 2 * tile_ids + chosen
    return (logical % devices * per_device + logical // devices).astype(jnp.int32)


def draw_row_maps(key, part):
    return jnp.stack([cyclic_law(jax.random.fold_in(key, 21 + child_id), CRB, N_ROW // 2, N_ROW, PRB) for child_id in range(2)])


def draw_col_maps(key, part):
    return jnp.stack([cyclic_law(jax.random.fold_in(key, 31 + child_id), KC, N_COL // 2, N_COL, PC) for child_id in range(2)])


def draw_pairs(key, part):
    total = PT * PT
    cells = jnp.arange(total, dtype=jnp.int32)
    device = cells // PT // PRB * N_COL + cells % PT // PC
    hot_count = max(1, NPAIRS // (3 * PRB * PC))
    ranking = jax.random.permutation(jax.random.fold_in(key, 3), N_ROW * N_COL).astype(jnp.int32)
    hotter = (ranking[device] < hot_count).astype(jnp.int32)
    scores = jax.random.randint(jax.random.fold_in(key, 4), (total,), 0, 32768, dtype=jnp.int32) * total + cells + hotter * 1073741824
    unused, chosen = lax.top_k(scores, NPAIRS)
    chosen = chosen.astype(jnp.int32)
    return jnp.stack([chosen // PT, chosen % PT], axis=1).astype(jnp.int32)


def block_levels(own_key, extent, cuts, least, top_value):
    level = 1.0
    for dim, blocks in cuts:
        heights = jax.random.uniform(jax.random.fold_in(jax.random.fold_in(own_key, 6), dim), (blocks,), jnp.float32, least / len(cuts), top_value / len(cuts))
        level = level * jnp.repeat(jnp.exp(heights), extent[dim] // blocks).reshape((-1,) + (1,) * (len(extent) - 1 - dim))
    return level


def bell_draw(stream_key, dims, scale, limit, shards=(), kind=jnp.bfloat16):
    array = jax.random.normal(stream_key, dims, jnp.float32) * scale
    if len(shards) > 0:
        array = block_levels(stream_key, dims, shards, -0.22, 0.18) * array
    return jnp.clip(array, min=-limit, max=limit).astype(kind)


def setup_inputs(seed: int = 0) -> dict:
    key_of = jax.random.split(jax.random.key(seed), 7)
    return {
        "children": bell_draw(key_of[0], (2 * C, C), 1.0, 6.0, ((0, 8), (1, 16))),
        "row_maps": draw_row_maps(jax.random.fold_in(key_of[6], 71), 0),
        "col_maps": draw_col_maps(jax.random.fold_in(key_of[6], 71), 0),
        "pairs": draw_pairs(jax.random.fold_in(key_of[6], 71), 0),
        "lower_panel": bell_draw(key_of[4], (P_SIZE, K), 1.0, 6.0, ((0, 8), (1, 16))),
        "upper_panel": bell_draw(key_of[5], (K, P_SIZE), K ** -0.5, 0.1875, ((0, 8), (1, 16))),
    }


def reference(children, row_maps, col_maps, pairs, lower_panel, upper_panel):
    tile_count = C // TILE
    parent_count = 2 * tile_count
    front_tiles = jnp.zeros((parent_count, TILE, parent_count, TILE), jnp.float32)
    for child_id in range(2):
        child_block = children[child_id * C:(child_id + 1) * C].astype(jnp.float32)
        child_block = child_block.reshape(tile_count, TILE, tile_count, TILE).transpose(0, 2, 1, 3)
        front_tiles = front_tiles.at[row_maps[child_id][:, None], :, col_maps[child_id][None, :], :].add(child_block)
    lower_tiles = lower_panel.astype(jnp.float32).reshape(parent_count, TILE, K)
    upper_tiles = upper_panel.astype(jnp.float32).reshape(K, parent_count, TILE).transpose(1, 0, 2)
    groups = pairs.reshape(NPAIRS // 32, 32, 2)

    def product(pair_group):
        return jnp.einsum("nik,nkj->nij", lower_tiles[pair_group[:, 0]], upper_tiles[pair_group[:, 1]], precision=lax.Precision.HIGHEST)

    updates = lax.map(product, groups).reshape(NPAIRS, TILE, TILE)
    front_tiles = front_tiles.at[pairs[:, 0], :, pairs[:, 1], :].add(-updates)
    return front_tiles.reshape(parent_count * TILE, parent_count * TILE)
```

```python
import functools

import jax
import jax.numpy as jnp
import numpy as np
from jax import lax
from jax.experimental import pallas as pl
from jax.experimental.pallas import tpu as pltpu
from jax.sharding import PartitionSpec as P

TILE = 128
COLS = 16
ROWS = 8
XS = 4
CT = 80
KC = 5
KR = 5
PRB = 20
PC = 10
ROUNDS = 5


def column_plan():
    holder = {}
    for m in range(8):
        side = []
        for k in range(PC):
            z = (m + 8 * k) // KC % 4
            if z // 2 == m % 2:
                side.append(z % 2)
            else:
                side.append({1: 0, 2: 1, 0: 1, 3: 0}[z])
        while sum(side) != ROUNDS:
            heavy = 0 if sum(side) < ROUNDS else 1
            for k in range(PC):
                z = (m + 8 * k) // KC % 4
                if side[k] == heavy and z // 2 == m % 2:
                    side[k] = 1 - heavy
                    break
        for k in range(PC):
            holder[m + 8 * k] = 2 * m + side[k]
    left = set(range(CT))
    rounds = []
    for _ in range(ROUNDS):
        owner = {}

        def place(source, seen):
            for j in range(source * KC, source * KC + KC):
                target = holder[j]
                if j not in left or target in seen:
                    continue
                seen.add(target)
                if target not in owner or place(owner[target] // KC, seen):
                    owner[target] = j
                    return True
            return False

        for source in range(COLS):
            assert place(source, set())
        rounds.append(dict(owner))
        left -= set(owner.values())
    assert not left
    return rounds


def pack_kernel(where, children, *outs):
    for r in range(ROUNDS):
        start = pl.multiple_of(where[XS + r] * TILE, TILE)
        for g in range(XS):
            for kk in range(KR):
                outs[r * XS + g][kk] = children[kk, where[g], :, pl.ds(start, TILE)]


def pack(children, where):
    spec = pltpu.PrefetchScalarGridSpec(
        num_scalar_prefetch=1,
        grid=(1,),
        in_specs=[pl.BlockSpec((KR, XS, TILE, KC * TILE), lambda i, w: (0, 0, 0, 0))],
        out_specs=[pl.BlockSpec((KR, TILE, TILE), lambda i, w: (0, 0, 0))] * (ROUNDS * XS),
    )
    return pl.pallas_call(
        pack_kernel,
        grid_spec=spec,
        out_shape=[jax.ShapeDtypeStruct((KR, TILE, TILE), jnp.bfloat16)] * (ROUNDS * XS),
        compiler_params=pltpu.CompilerParams(vmem_limit_bytes=32 << 20),
        cost_estimate=pl.CostEstimate(flops=0, bytes_accessed=6553600, transcendentals=0),
        name="pack",
    )(where, children.reshape(KR, XS, TILE, KC * TILE))


CORE, X_LO, X_HI, SLOT, COL_ON, ROW_ON = 0, 1, 2, 4, 14, 34


def front_kernel(scal, listed, lower, upper, *refs):
    units, out = refs[:-1], refs[-1]
    block = pl.program_id(0)
    same = block % 2 == scal[CORE]
    x_hi = scal[X_HI]

    for kk in range(KR):
        rows = pl.ds(kk * TILE, TILE)
        acc = jnp.dot(lower[rows, :], upper[...], preferred_element_type=jnp.float32)
        out[rows, :] = jnp.where(listed[block * KR + kk] > 0.5, -acc, 0.0)

    def add(refs):
        for w in range(2):
            for r in range(ROUNDS):
                ref = refs[w * ROUNDS + r]
                start = pl.multiple_of(scal[SLOT + w * ROUNDS + r] * TILE, TILE)
                for g in range(2):
                    child = g ^ x_hi

                    @pl.when(scal[COL_ON + (w * ROUNDS + r) * 2 + g] == 1)
                    def _():
                        for kk in range(KR):

                            @pl.when(scal[ROW_ON + child * PRB + block * KR + kk] == 1)
                            def _():
                                rows = pl.ds(kk * TILE, TILE)
                                out[rows, pl.ds(start, TILE)] += ref[g, 0, kk].astype(jnp.float32)

    @pl.when(same)
    def _():
        add(units[: 2 * ROUNDS])

    @pl.when(jnp.logical_not(same))
    def _():
        add(units[2 * ROUNDS :])


def front(scal, listed, lower, upper, units):
    def own_map(b, s):
        half = jnp.where(s[CORE] == b % 2, b // 2, jnp.maximum(b - 1, 0) // 2)
        return (0, half ^ s[X_LO], 0, 0, 0)

    def other_map(b, s):
        half = jnp.where(s[CORE] != b % 2, b // 2, jnp.maximum(b - 1, 0) // 2)
        return (0, half ^ s[X_LO], 0, 0, 0)

    unit = (2, 1, KR, TILE, TILE)
    height = KR * TILE
    spec = pltpu.PrefetchScalarGridSpec(
        num_scalar_prefetch=1,
        grid=(PRB // KR,),
        in_specs=[
            pl.BlockSpec((PRB, 1, PC * TILE), lambda b, s: (0, 0, 0)),
            pl.BlockSpec((height, 1024), lambda b, s: (b, 0)),
            pl.BlockSpec((1024, PC * TILE), lambda b, s: (0, 0)),
        ]
        + [pl.BlockSpec(unit, own_map)] * (2 * ROUNDS)
        + [pl.BlockSpec(unit, other_map)] * (2 * ROUNDS),
        out_specs=pl.BlockSpec((height, PC * TILE), lambda b, s: (b, 0)),
    )
    return pl.pallas_call(
        front_kernel,
        grid_spec=spec,
        out_shape=jax.ShapeDtypeStruct((PRB * TILE, PC * TILE), jnp.float32),
        compiler_params=pltpu.CompilerParams(vmem_limit_bytes=56 << 20),
        cost_estimate=pl.CostEstimate(
            flops=2 * 2560 * 1280 * 1024, bytes_accessed=34 << 20, transcendentals=0
        ),
        name="front",
    )(scal, listed, lower, upper, *units)


def body(children, row_maps, col_maps, pairs, lower_panel, upper_panel):
    row = lax.axis_index("row")
    col = lax.axis_index("col")
    chip, core = row // 2, row % 2
    rounds = column_plan()
    source_of = [[0] * COLS for _ in range(ROUNDS)]
    tile_of = np.zeros((ROUNDS, COLS), np.int32)
    slot_of = np.zeros((ROUNDS, COLS), np.int32)
    for r, owner in enumerate(rounds):
        for target, j in owner.items():
            source_of[r][target] = j // KC
            tile_of[r, j // KC] = j % KC
            slot_of[r, target] = j // 8

    lower_all = lax.all_gather(lower_panel.T, "col", axis=0, tiled=True)
    upper_all = lax.all_gather(upper_panel, "row", axis=0, tiled=True)

    where = jnp.concatenate(
        [chip ^ jnp.arange(XS, dtype=jnp.int32), jnp.asarray(tile_of)[:, col]]
    ).astype(jnp.int32)
    packed = pack(children, where)

    held, swapped, core_held, core_swapped = [], [], [], []
    for r in range(ROUNDS):
        sent = packed[r * XS : (r + 1) * XS]
        if r > 0:
            sent, held[r - 1] = lax.optimization_barrier((sent, held[r - 1]))
        got = []
        for g in range(XS):
            route = [
                (p * COLS + source_of[r][q], (p ^ (2 * g)) * COLS + q)
                for p in range(ROWS)
                for q in range(COLS)
            ]
            got.append(lax.ppermute(sent[g], ("row", "col"), route))
        held.append(jnp.stack(got).reshape(2, 2, KR, TILE, TILE))
    for r in range(ROUNDS):
        swapped.append(lax.ppermute(held[r], "col", [(q, q ^ 1) for q in range(COLS)]))
        core_held.append(lax.ppermute(held[r], "row", [(p, p ^ 1) for p in range(ROWS)]))
        core_swapped.append(lax.ppermute(swapped[r], "row", [(p, p ^ 1) for p in range(ROWS)]))

    slots = jnp.arange(PRB, dtype=jnp.int32)
    row_on = lax.dynamic_slice_in_dim(row_maps.reshape(2, PRB, XS), chip, 1, 2)[:, :, 0]
    row_on = (row_on == row * PRB + slots).astype(jnp.int32)
    spots = jnp.arange(PC, dtype=jnp.int32)
    col_on = lax.dynamic_slice_in_dim(col_maps.reshape(2, PC, 8), col // 2, 1, 2)[:, :, 0]
    col_on = (col_on == col * PC + spots).astype(jnp.int32)
    slot = jnp.concatenate([jnp.asarray(slot_of)[:, col], jnp.asarray(slot_of)[:, col ^ 1]])
    sides = (chip // 2) ^ jnp.arange(2, dtype=jnp.int32)
    by_slot = jnp.sum(
        jnp.where(slot[:, None] == spots[None, :], 1, 0)[:, None, :] * col_on[sides][None], axis=2
    )
    scal = jnp.concatenate(
        [
            jnp.stack([core, chip % 2, chip // 2, chip]),
            slot,
            by_slot.reshape(-1),
            row_on.reshape(-1),
        ]
    ).astype(jnp.int32)

    row_hit = (pairs[:, 0][:, None] == row * PRB + slots[None, :]).astype(jnp.bfloat16)
    col_hit = (pairs[:, 1][:, None] == col * PC + spots[None, :]).astype(jnp.bfloat16)
    listed = jnp.dot(row_hit.T, col_hit, preferred_element_type=jnp.float32)
    listed = jnp.repeat(listed, TILE, axis=1).reshape(PRB, 1, PC * TILE)

    return front(
        scal, listed, lower_all.T, upper_all, held + swapped + core_held + core_swapped
    )


def solution(mesh):
    placed = (P("row", "col"), P(), P(), P(), P("row", "col"), P("row", "col"))
    return jax.shard_map(
        body, mesh=mesh, in_specs=placed, out_specs=P("row", "col"), check_vma=False
    )
```

```python
import jax
import jax.numpy as jnp
import numpy as np
from jax import lax
from jax.experimental import pallas as pl
from jax.experimental.pallas import tpu as pltpu
from jax.sharding import PartitionSpec as P


TILE = 128
COLS = 16
ROWS = 8
XS = 4
CT = 80
KC = 5
KR = 5
PRB = 20
PC = 10
ROUNDS = 5


def column_plan():
    holder, crossing, taken = {}, [], set()
    for m in range(8):
        side = []
        for k in range(PC):
            z = (m + 8 * k) // KC % 4
            if z // 2 == m % 2:
                side.append(z % 2)
            else:
                side.append({1: 0, 2: 1, 0: 1, 3: 0}[z])
        while sum(side) != ROUNDS:
            heavy = 0 if sum(side) < ROUNDS else 1
            for k in range(PC):
                z = (m + 8 * k) // KC % 4
                source = (m + 8 * k) // KC
                if side[k] == heavy and z // 2 == m % 2 and source not in taken:
                    side[k] = 1 - heavy
                    taken.add(source)
                    crossing.append(m + 8 * k)
                    break
        for k in range(PC):
            holder[m + 8 * k] = 2 * m + side[k]
    left = set(range(CT))
    rounds = []
    for r in range(ROUNDS):
        owner = {holder[j]: j for j in crossing} if r == 0 else {}
        fixed = {j // KC for j in owner.values()}

        def place(source, seen):
            for j in range(source * KC, source * KC + KC):
                target = holder[j]
                if j not in left or target in seen:
                    continue
                seen.add(target)
                free = target not in owner
                if not free and owner[target] // KC in fixed:
                    continue
                if free or place(owner[target] // KC, seen):
                    owner[target] = j
                    return True
            return False

        for source in range(COLS):
            assert source in fixed or place(source, set())
        rounds.append(dict(owner))
        left -= set(owner.values())
    assert not left
    return rounds


def pack_kernel(where, children, *outs):
    for r in range(ROUNDS):
        start = pl.multiple_of(where[XS + r] * TILE, TILE)
        for g in range(XS):
            for kk in range(KR):
                outs[r * XS + g][kk] = children[kk, where[g], :, pl.ds(start, TILE)]


def pack(children, where):
    spec = pltpu.PrefetchScalarGridSpec(
        num_scalar_prefetch=1,
        grid=(1,),
        in_specs=[pl.BlockSpec((KR, XS, TILE, KC * TILE), lambda i, w: (0, 0, 0, 0))],
        out_specs=[pl.BlockSpec((KR, TILE, TILE), lambda i, w: (0, 0, 0))] * (ROUNDS * XS),
    )
    return pl.pallas_call(
        pack_kernel,
        grid_spec=spec,
        out_shape=[jax.ShapeDtypeStruct((KR, TILE, TILE), jnp.bfloat16)] * (ROUNDS * XS),
        compiler_params=pltpu.CompilerParams(vmem_limit_bytes=32 << 20),
        cost_estimate=pl.CostEstimate(flops=0, bytes_accessed=6553600, transcendentals=0),
        name="pack",
    )(where, children.reshape(KR, XS, TILE, KC * TILE))


CORE, X_LO, X_HI, SLOT, COL_ON, ROW_ON = 0, 1, 2, 4, 14, 34
UNIT = (2, 1, KR, TILE, TILE)
HEIGHT = KR * TILE


def half_of(matches, block, scal):
    return jnp.where(matches, block // 2, jnp.maximum(block - 1, 0) // 2) ^ scal[X_LO]


def own_map(b, s):
    return (0, half_of(s[CORE] == b % 2, b, s), 0, 0, 0)


def other_map(b, s):
    return (0, half_of(s[CORE] != b % 2, b, s), 0, 0, 0)


def add_unit(scal, spot, block, unit, out, start):
    for g in range(2):
        child = g ^ scal[X_HI]

        @pl.when(scal[COL_ON + spot * 2 + g] == 1)
        def _():
            for kk in range(KR):

                @pl.when(scal[ROW_ON + child * PRB + block * KR + kk] == 1)
                def _():
                    rows = pl.ds(kk * TILE, TILE)
                    out[rows, pl.ds(start, TILE)] += unit[g, 0, kk].astype(jnp.float32)


def base_kernel(spots, scal, listed, lower, upper, *refs):
    units, out = refs[:-1], refs[-1]
    block = pl.program_id(0)
    same = block % 2 == scal[CORE]
    for kk in range(KR):
        rows = pl.ds(kk * TILE, TILE)
        acc = jnp.dot(lower[rows, :], upper[...], preferred_element_type=jnp.float32)
        out[rows, :] = jnp.where(listed[block * KR + kk] > 0.5, -acc, 0.0)

    def add(group):
        for spot, unit in zip(spots, group):
            start = pl.multiple_of(scal[SLOT + spot] * TILE, TILE)
            add_unit(scal, spot, block, unit, out, start)

    @pl.when(same)
    def _():
        add(units[: len(spots)])

    @pl.when(jnp.logical_not(same))
    def _():
        add(units[len(spots) :])


def base(scal, listed, lower, upper, spots, own, other):
    n = len(spots)
    spec = pltpu.PrefetchScalarGridSpec(
        num_scalar_prefetch=1,
        grid=(PRB // KR,),
        in_specs=[
            pl.BlockSpec((PRB, 1, PC * TILE), lambda b, s: (0, 0, 0)),
            pl.BlockSpec((HEIGHT, 1024), lambda b, s: (b, 0)),
            pl.BlockSpec((1024, PC * TILE), lambda b, s: (0, 0)),
        ]
        + [pl.BlockSpec(UNIT, own_map)] * n
        + [pl.BlockSpec(UNIT, other_map)] * n,
        out_specs=pl.BlockSpec((HEIGHT, PC * TILE), lambda b, s: (b, 0)),
    )

    def kernel(*refs):
        base_kernel(spots, *refs)

    return pl.pallas_call(
        kernel,
        grid_spec=spec,
        out_shape=jax.ShapeDtypeStruct((PRB * TILE, PC * TILE), jnp.float32),
        compiler_params=pltpu.CompilerParams(vmem_limit_bytes=56 << 20),
        cost_estimate=pl.CostEstimate(
            flops=2 * 2560 * 1280 * 1024, bytes_accessed=34 << 20, transcendentals=0
        ),
        name="base",
    )(scal, listed, lower, upper, *own, *other)


def tail(scal, front, spots, own, other):
    n = len(spots)

    def kernel(scal, *refs):
        units, fronts, out = refs[: 2 * n], refs[2 * n], refs[2 * n + 1]
        block = pl.program_id(1)
        same = block % 2 == scal[CORE]
        out[...] = fronts[...]
        for i, spot in enumerate(spots):

            @pl.when((pl.program_id(0) == i) & same)
            def _():
                add_unit(scal, spot, block, units[i], out, 0)

            @pl.when((pl.program_id(0) == i) & jnp.logical_not(same))
            def _():
                add_unit(scal, spot, block, units[n + i], out, 0)

    def front_map(i, b, s):
        slot = s[SLOT + spots[0]]
        for j in range(1, n):
            slot = jnp.where(i == j, s[SLOT + spots[j]], slot)
        return (b, slot)

    def unit_map(index, pick):
        def at(i, b, s):
            now = jnp.where(i == index, b, jnp.where(i < index, 0, PRB // KR - 1))
            return pick(now, s)

        return at

    spec = pltpu.PrefetchScalarGridSpec(
        num_scalar_prefetch=1,
        grid=(n, PRB // KR),
        in_specs=[pl.BlockSpec(UNIT, unit_map(i, own_map)) for i in range(n)]
        + [pl.BlockSpec(UNIT, unit_map(i, other_map)) for i in range(n)]
        + [pl.BlockSpec((HEIGHT, TILE), front_map)],
        out_specs=pl.BlockSpec((HEIGHT, TILE), front_map),
    )
    return pl.pallas_call(
        kernel,
        grid_spec=spec,
        out_shape=jax.ShapeDtypeStruct((PRB * TILE, PC * TILE), jnp.float32),
        input_output_aliases={2 * n + 1: 0},
        compiler_params=pltpu.CompilerParams(vmem_limit_bytes=32 << 20),
        cost_estimate=pl.CostEstimate(flops=0, bytes_accessed=8 << 20, transcendentals=0),
        name="tail",
    )(scal, *own, *other, front)


def hop(array, row_mask=0, col_mask=0):
    route = [
        (p * COLS + q, (p ^ row_mask) * COLS + (q ^ col_mask))
        for p in range(ROWS)
        for q in range(COLS)
    ]
    return lax.ppermute(array, ("row", "col"), route)


def compute(children, row_maps, col_maps, pairs, lower_panel, upper_panel):
    row = lax.axis_index("row")
    col = lax.axis_index("col")
    chip, core = row >> 1, row & 1
    rounds = column_plan()
    source_of = [[0] * COLS for _ in range(ROUNDS)]
    tile_of = np.zeros((ROUNDS, COLS), np.int32)
    slot_of = np.zeros((ROUNDS, COLS), np.int32)
    for r, owner in enumerate(rounds):
        for target, j in owner.items():
            source_of[r][target] = j // KC
            tile_of[r, j // KC] = j % KC
            slot_of[r, target] = j // 8

    low = lower_panel.T
    low_z1 = hop(low, col_mask=1)
    low01 = jnp.concatenate([low, low_z1])
    low32 = hop(low01, col_mask=3)
    low_here = jnp.concatenate([low01, low32])
    low_y1 = hop(low_here, col_mask=4)
    low_y3 = hop(low_here, col_mask=12)
    low_y2a = hop(low_y1[:128], col_mask=12)
    low_y2b = hop(low_y3[128:], col_mask=4)
    lower_all = jnp.concatenate([low_here, low_y1, low_y2a, low_y2b, low_y3]).T
    piece_col = col ^ (
        4 * jnp.asarray([0, 1, 2, 3], jnp.int32)[:, None]
        + jnp.asarray([0, 1, 3, 2], jnp.int32)[None, :]
    ).reshape(-1)

    up_x1 = hop(upper_panel, row_mask=2)
    up01 = jnp.concatenate([upper_panel, up_x1])
    up32 = hop(up01, row_mask=6)
    up_here = jnp.concatenate([up01, up32])
    up_core = hop(up_here, row_mask=1)
    up_pieces = jnp.concatenate([up_here, up_core]).reshape(2, XS, 2, 64, PC * TILE)
    piece_row = row ^ (piece_col >> 1)
    flip = piece_row >> 1
    place = jnp.where(flip == 2, 3, jnp.where(flip == 3, 2, flip))
    index = ((piece_row & 1) * XS + place) * 2 + (piece_col & 1)
    upper_all = jnp.take(up_pieces.reshape(16, 64, PC * TILE), index, axis=0, mode="clip")
    upper_all = upper_all.reshape(1024, PC * TILE)

    where = jnp.concatenate(
        [chip ^ jnp.arange(XS, dtype=jnp.int32), jnp.asarray(tile_of)[:, col]]
    ).astype(jnp.int32)
    packed = pack(children, where)

    held, swapped, core_held, core_swapped = [], [], [], []
    for r in range(ROUNDS):
        got = []
        for g in range(XS):
            route = [
                (p * COLS + source_of[r][q], (p ^ (2 * g)) * COLS + q)
                for p in range(ROWS)
                for q in range(COLS)
            ]
            got.append(lax.ppermute(packed[r * XS + g], ("row", "col"), route))
        held.append(jnp.stack(got).reshape(2, 2, KR, TILE, TILE))
    for r in range(ROUNDS):
        swapped.append(hop(held[r], col_mask=1))
        core_held.append(hop(held[r], row_mask=1))
        core_swapped.append(hop(swapped[r], row_mask=1))

    slots = jnp.arange(PRB, dtype=jnp.int32)
    row_on = lax.dynamic_slice_in_dim(row_maps.reshape(2, PRB, XS), chip, 1, 2)[:, :, 0]
    row_on = (row_on == row * PRB + slots).astype(jnp.int32)
    spots = jnp.arange(PC, dtype=jnp.int32)
    col_on = lax.dynamic_slice_in_dim(col_maps.reshape(2, PC, 8), col >> 1, 1, 2)[:, :, 0]
    col_on = (col_on == col * PC + spots).astype(jnp.int32)
    slot = jnp.concatenate([jnp.asarray(slot_of)[:, col], jnp.asarray(slot_of)[:, col ^ 1]])
    sides = (chip >> 1) ^ jnp.arange(2, dtype=jnp.int32)
    by_slot = jnp.sum(
        jnp.where(slot[:, None] == spots[None, :], 1, 0)[:, None, :] * col_on[sides][None], axis=2
    )
    scal = jnp.concatenate(
        [
            jnp.stack([core, chip & 1, chip >> 1, chip]),
            slot,
            by_slot.reshape(-1),
            row_on.reshape(-1),
        ]
    ).astype(jnp.int32)

    row_hit = (pairs[:, 0][:, None] == row * PRB + slots[None, :]).astype(jnp.bfloat16)
    col_hit = (pairs[:, 1][:, None] == col * PC + spots[None, :]).astype(jnp.bfloat16)
    listed = jnp.dot(row_hit.T, col_hit, preferred_element_type=jnp.float32)
    listed = jnp.repeat(listed, TILE, axis=1).reshape(PRB, 1, PC * TILE)

    own = held + swapped
    other = core_held + core_swapped
    early = list(range(2 * ROUNDS - 2))
    late = [2 * ROUNDS - 2, 2 * ROUNDS - 1]
    front = base(
        scal,
        listed,
        lower_all,
        upper_all,
        early,
        [own[i] for i in early],
        [other[i] for i in early],
    )
    return tail(scal, front, late, [own[i] for i in late], [other[i] for i in late])


def solution(mesh):
    placed = (P("row", "col"), P(), P(), P(), P("row", "col"), P("row", "col"))
    return jax.shard_map(
        compute, mesh=mesh, in_specs=placed, out_specs=P("row", "col"), check_vma=False
    )
```

```python
import jax
import jax.numpy as jnp
import numpy as np
from jax import lax
from jax.experimental import pallas as pl
from jax.experimental.pallas import tpu as pltpu
from jax.sharding import PartitionSpec as P


TILE = 128
COLS = 16
ROWS = 8
XS = 4
CT = 80
KC = 5
KR = 5
PRB = 20
PC = 10
ROUNDS = 5


def column_plan():
    holder, crossing, taken = {}, [], set()
    for m in range(8):
        side = []
        for k in range(PC):
            z = (m + 8 * k) // KC % 4
            if z // 2 == m % 2:
                side.append(z % 2)
            else:
                side.append({1: 0, 2: 1, 0: 1, 3: 0}[z])
        while sum(side) != ROUNDS:
            heavy = 0 if sum(side) < ROUNDS else 1
            for k in range(PC):
                z = (m + 8 * k) // KC % 4
                source = (m + 8 * k) // KC
                if side[k] == heavy and z // 2 == m % 2 and source not in taken:
                    side[k] = 1 - heavy
                    taken.add(source)
                    crossing.append(m + 8 * k)
                    break
        for k in range(PC):
            holder[m + 8 * k] = 2 * m + side[k]
    left = set(range(CT))
    rounds = []
    for r in range(ROUNDS):
        owner = {holder[j]: j for j in crossing} if r == 0 else {}
        fixed = {j // KC for j in owner.values()}

        def place(source, seen):
            for j in range(source * KC, source * KC + KC):
                target = holder[j]
                if j not in left or target in seen:
                    continue
                seen.add(target)
                free = target not in owner
                if not free and owner[target] // KC in fixed:
                    continue
                if free or place(owner[target] // KC, seen):
                    owner[target] = j
                    return True
            return False

        for source in range(COLS):
            assert source in fixed or place(source, set())
        rounds.append(dict(owner))
        left -= set(owner.values())
    assert not left
    return rounds


def pack_kernel(where, children, *outs):
    for r in range(ROUNDS):
        start = pl.multiple_of(where[r] * TILE, TILE)
        for x in range(XS):
            for kk in range(KR):
                outs[r][x, kk] = children[kk, x, :, pl.ds(start, TILE)]


def pack(children, where):
    spec = pltpu.PrefetchScalarGridSpec(
        num_scalar_prefetch=1,
        grid=(1,),
        in_specs=[pl.BlockSpec((KR, XS, TILE, KC * TILE), lambda i, w: (0, 0, 0, 0))],
        out_specs=[pl.BlockSpec((XS, KR, TILE, TILE), lambda i, w: (0, 0, 0, 0))] * ROUNDS,
    )
    return pl.pallas_call(
        pack_kernel,
        grid_spec=spec,
        out_shape=[jax.ShapeDtypeStruct((XS, KR, TILE, TILE), jnp.bfloat16)] * ROUNDS,
        compiler_params=pltpu.CompilerParams(vmem_limit_bytes=32 << 20),
        cost_estimate=pl.CostEstimate(flops=0, bytes_accessed=6553600, transcendentals=0),
        name="pack",
    )(where, children.reshape(KR, XS, TILE, KC * TILE))


CORE, SLOT, COL_ON, ROW_ON = 0, 1, 11, 31
UNIT = (2, 1, KR, TILE, TILE)
HEIGHT = KR * TILE


def half_of(matches, block):
    return jnp.where(matches, block // 2, jnp.maximum(block - 1, 0) // 2)


def own_map(b, s):
    return (0, half_of(s[CORE] == b % 2, b), 0, 0, 0)


def other_map(b, s):
    return (0, half_of(s[CORE] != b % 2, b), 0, 0, 0)


def add_unit(scal, spot, block, unit, out, start):
    for child in range(2):

        @pl.when(scal[COL_ON + spot * 2 + child] == 1)
        def _():
            for kk in range(KR):

                @pl.when(scal[ROW_ON + child * PRB + block * KR + kk] == 1)
                def _():
                    rows = pl.ds(kk * TILE, TILE)
                    out[rows, pl.ds(start, TILE)] += unit[child, 0, kk].astype(jnp.float32)


def base_kernel(spots, scal, listed, lower, upper, *refs):
    units, out = refs[:-1], refs[-1]
    block = pl.program_id(0)
    same = block % 2 == scal[CORE]
    for kk in range(KR):
        rows = pl.ds(kk * TILE, TILE)
        acc = jnp.dot(lower[rows, :], upper[...], preferred_element_type=jnp.float32)
        out[rows, :] = jnp.where(listed[block * KR + kk] > 0.5, -acc, 0.0)

    def add(group):
        for spot, unit in zip(spots, group):
            start = pl.multiple_of(scal[SLOT + spot] * TILE, TILE)
            add_unit(scal, spot, block, unit, out, start)

    @pl.when(same)
    def _():
        add(units[: len(spots)])

    @pl.when(jnp.logical_not(same))
    def _():
        add(units[len(spots) :])


def base(scal, listed, lower, upper, spots, own, other):
    n = len(spots)
    spec = pltpu.PrefetchScalarGridSpec(
        num_scalar_prefetch=1,
        grid=(PRB // KR,),
        in_specs=[
            pl.BlockSpec((PRB, 1, PC * TILE), lambda b, s: (0, 0, 0)),
            pl.BlockSpec((HEIGHT, 1024), lambda b, s: (b, 0)),
            pl.BlockSpec((1024, PC * TILE), lambda b, s: (0, 0)),
        ]
        + [pl.BlockSpec(UNIT, own_map)] * n
        + [pl.BlockSpec(UNIT, other_map)] * n,
        out_specs=pl.BlockSpec((HEIGHT, PC * TILE), lambda b, s: (b, 0)),
    )

    def kernel(*refs):
        base_kernel(spots, *refs)

    return pl.pallas_call(
        kernel,
        grid_spec=spec,
        out_shape=jax.ShapeDtypeStruct((PRB * TILE, PC * TILE), jnp.float32),
        compiler_params=pltpu.CompilerParams(vmem_limit_bytes=56 << 20),
        cost_estimate=pl.CostEstimate(
            flops=2 * 2560 * 1280 * 1024, bytes_accessed=34 << 20, transcendentals=0
        ),
        name="base",
    )(scal, listed, lower, upper, *own, *other)


def tail(scal, front, spots, own, other):
    n = len(spots)

    def kernel(scal, *refs):
        units, fronts, out = refs[: 2 * n], refs[2 * n], refs[2 * n + 1]
        block = pl.program_id(1)
        same = block % 2 == scal[CORE]
        out[...] = fronts[...]
        for i, spot in enumerate(spots):

            @pl.when((pl.program_id(0) == i) & same)
            def _():
                add_unit(scal, spot, block, units[i], out, 0)

            @pl.when((pl.program_id(0) == i) & jnp.logical_not(same))
            def _():
                add_unit(scal, spot, block, units[n + i], out, 0)

    def front_map(i, b, s):
        slot = s[SLOT + spots[0]]
        for j in range(1, n):
            slot = jnp.where(i == j, s[SLOT + spots[j]], slot)
        return (b, slot)

    def unit_map(index, pick):
        def at(i, b, s):
            now = jnp.where(i == index, b, jnp.where(i < index, 0, PRB // KR - 1))
            return pick(now, s)

        return at

    spec = pltpu.PrefetchScalarGridSpec(
        num_scalar_prefetch=1,
        grid=(n, PRB // KR),
        in_specs=[pl.BlockSpec(UNIT, unit_map(i, own_map)) for i in range(n)]
        + [pl.BlockSpec(UNIT, unit_map(i, other_map)) for i in range(n)]
        + [pl.BlockSpec((HEIGHT, TILE), front_map)],
        out_specs=pl.BlockSpec((HEIGHT, TILE), front_map),
    )
    return pl.pallas_call(
        kernel,
        grid_spec=spec,
        out_shape=jax.ShapeDtypeStruct((PRB * TILE, PC * TILE), jnp.float32),
        input_output_aliases={2 * n + 1: 0},
        compiler_params=pltpu.CompilerParams(vmem_limit_bytes=32 << 20),
        cost_estimate=pl.CostEstimate(flops=0, bytes_accessed=8 << 20, transcendentals=0),
        name="tail",
    )(scal, *own, *other, front)


def hop(array, row_mask=0, col_mask=0):
    route = [
        (p * COLS + q, (p ^ row_mask) * COLS + (q ^ col_mask))
        for p in range(ROWS)
        for q in range(COLS)
    ]
    return lax.ppermute(array, ("row", "col"), route)


def compute(children, row_maps, col_maps, pairs, lower_panel, upper_panel):
    row = lax.axis_index("row")
    col = lax.axis_index("col")
    chip, core = row >> 1, row & 1
    rounds = column_plan()
    source_of = [[0] * COLS for _ in range(ROUNDS)]
    tile_of = np.zeros((ROUNDS, COLS), np.int32)
    slot_of = np.zeros((ROUNDS, COLS), np.int32)
    for r, owner in enumerate(rounds):
        for target, j in owner.items():
            source_of[r][target] = j // KC
            tile_of[r, j // KC] = j % KC
            slot_of[r, target] = j // 8

    along_z = [[4 * y + z for z in range(4)] for y in range(4)]
    along_y = [[4 * y + z for y in range(4)] for z in range(4)]
    lower_here = lax.all_gather(
        lower_panel.T, "col", axis=0, tiled=True, axis_index_groups=along_z
    )
    upper_all = lax.all_gather(upper_panel, "row", axis=0, tiled=True)

    packed = pack(children, jnp.asarray(tile_of)[:, col])

    held, swapped, core_held, core_swapped = [], [], [], []
    same_core = [[2 * x + c for x in range(XS)] for c in range(2)]
    for r in range(ROUNDS):
        got = lax.all_to_all(
            packed[r], "row", 0, 0, axis_index_groups=same_core, tiled=True
        )
        if r == 1:
            lower_here, got = lax.optimization_barrier((lower_here, got))
            lower_all = lax.all_gather(
                lower_here, "col", axis=0, tiled=True, axis_index_groups=along_y
            ).T
        got = lax.ppermute(got, "col", [(source_of[r][q], q) for q in range(COLS)])
        held.append(got.reshape(UNIT[0], 2, KR, TILE, TILE))
    for r in range(ROUNDS):
        swapped.append(hop(held[r], col_mask=1))
        core_held.append(hop(held[r], row_mask=1))
        core_swapped.append(hop(swapped[r], row_mask=1))

    slots = jnp.arange(PRB, dtype=jnp.int32)
    row_on = lax.dynamic_slice_in_dim(row_maps.reshape(2, PRB, XS), chip, 1, 2)[:, :, 0]
    row_on = (row_on == row * PRB + slots).astype(jnp.int32)
    spots = jnp.arange(PC, dtype=jnp.int32)
    col_on = lax.dynamic_slice_in_dim(col_maps.reshape(2, PC, 8), col >> 1, 1, 2)[:, :, 0]
    col_on = (col_on == col * PC + spots).astype(jnp.int32)
    slot = jnp.concatenate([jnp.asarray(slot_of)[:, col], jnp.asarray(slot_of)[:, col ^ 1]])
    by_slot = jnp.sum(
        jnp.where(slot[:, None] == spots[None, :], 1, 0)[:, None, :] * col_on[None], axis=2
    )
    scal = jnp.concatenate(
        [
            core[None],
            slot,
            by_slot.reshape(-1),
            row_on.reshape(-1),
        ]
    ).astype(jnp.int32)

    row_hit = (pairs[:, 0][:, None] == row * PRB + slots[None, :]).astype(jnp.bfloat16)
    col_hit = (pairs[:, 1][:, None] == col * PC + spots[None, :]).astype(jnp.bfloat16)
    listed = jnp.dot(row_hit.T, col_hit, preferred_element_type=jnp.float32)
    listed = jnp.repeat(listed, TILE, axis=1).reshape(PRB, 1, PC * TILE)

    own = held + swapped
    other = core_held + core_swapped
    early = list(range(2 * ROUNDS - 2))
    late = [2 * ROUNDS - 2, 2 * ROUNDS - 1]
    front = base(
        scal,
        listed,
        lower_all,
        upper_all,
        early,
        [own[i] for i in early],
        [other[i] for i in early],
    )
    return tail(scal, front, late, [own[i] for i in late], [other[i] for i in late])


def solution(mesh):
    placed = (P("row", "col"), P(), P(), P(), P("row", "col"), P("row", "col"))
    return jax.shard_map(
        compute, mesh=mesh, in_specs=placed, out_specs=P("row", "col"), check_vma=False
    )
```

```python
import jax
import jax.numpy as jnp
import numpy as np
from jax import lax
from jax.experimental import pallas as pl
from jax.experimental.pallas import tpu as pltpu
from jax.sharding import PartitionSpec as P


TILE = 128
COLS = 16
ROWS = 8
XS = 4
CT = 80
KC = 5
KR = 5
PRB = 20
PC = 10
ROUNDS = 5


def column_plan():
    holder, crossing, taken = {}, [], set()
    for m in range(8):
        side = []
        for k in range(PC):
            z = (m + 8 * k) // KC % 4
            if z // 2 == m % 2:
                side.append(z % 2)
            else:
                side.append({1: 0, 2: 1, 0: 1, 3: 0}[z])
        while sum(side) != ROUNDS:
            heavy = 0 if sum(side) < ROUNDS else 1
            for k in range(PC):
                z = (m + 8 * k) // KC % 4
                source = (m + 8 * k) // KC
                if side[k] == heavy and z // 2 == m % 2 and source not in taken:
                    side[k] = 1 - heavy
                    taken.add(source)
                    crossing.append(m + 8 * k)
                    break
        for k in range(PC):
            holder[m + 8 * k] = 2 * m + side[k]
    left = set(range(CT))
    rounds = []
    for r in range(ROUNDS):
        owner = {holder[j]: j for j in crossing} if r == 0 else {}
        fixed = {j // KC for j in owner.values()}

        def place(source, seen):
            for j in range(source * KC, source * KC + KC):
                target = holder[j]
                if j not in left or target in seen:
                    continue
                seen.add(target)
                free = target not in owner
                if not free and owner[target] // KC in fixed:
                    continue
                if free or place(owner[target] // KC, seen):
                    owner[target] = j
                    return True
            return False

        for source in range(COLS):
            assert source in fixed or place(source, set())
        rounds.append(dict(owner))
        left -= set(owner.values())
    assert not left
    return rounds


def pack_kernel(where, children, *outs):
    for r in range(ROUNDS):
        start = pl.multiple_of(where[r] * TILE, TILE)
        for x in range(XS):
            for kk in range(KR):
                outs[r][x, kk] = children[kk, x, :, pl.ds(start, TILE)]


def pack(children, where):
    spec = pltpu.PrefetchScalarGridSpec(
        num_scalar_prefetch=1,
        grid=(1,),
        in_specs=[pl.BlockSpec((KR, XS, TILE, KC * TILE), lambda i, w: (0, 0, 0, 0))],
        out_specs=[pl.BlockSpec((XS, KR, TILE, TILE), lambda i, w: (0, 0, 0, 0))] * ROUNDS,
    )
    return pl.pallas_call(
        pack_kernel,
        grid_spec=spec,
        out_shape=[jax.ShapeDtypeStruct((XS, KR, TILE, TILE), jnp.bfloat16)] * ROUNDS,
        compiler_params=pltpu.CompilerParams(vmem_limit_bytes=32 << 20),
        cost_estimate=pl.CostEstimate(flops=0, bytes_accessed=6553600, transcendentals=0),
        name="pack",
    )(where, children.reshape(KR, XS, TILE, KC * TILE))


CORE, SLOT, COL_ON, ROW_ON, PIECE, IS_HERE = 0, 1, 11, 31, 71, 87
UNIT = (2, 1, KR, TILE, TILE)
HEIGHT = KR * TILE


def half_of(matches, block):
    return jnp.where(matches, block // 2, jnp.maximum(block - 1, 0) // 2)


def own_map(b, s):
    return (0, half_of(s[CORE] == b % 2, b), 0, 0, 0)


def other_map(b, s):
    return (0, half_of(s[CORE] != b % 2, b), 0, 0, 0)


def add_unit(scal, spot, block, unit, out, start):
    for child in range(2):

        @pl.when(scal[COL_ON + spot * 2 + child] == 1)
        def _():
            for kk in range(KR):

                @pl.when(scal[ROW_ON + child * PRB + block * KR + kk] == 1)
                def _():
                    rows = pl.ds(kk * TILE, TILE)
                    out[rows, pl.ds(start, TILE)] += unit[child, 0, kk].astype(jnp.float32)


def base_kernel(spots, scal, listed, *refs):
    lower, refs = refs[:8], refs[8:]
    up_here, up_core, units, out, upper = refs[0], refs[1], refs[2:-2], refs[-2], refs[-1]
    block = pl.program_id(0)
    same = block % 2 == scal[CORE]

    @pl.when(block == 0)
    def _():
        for i in range(COLS):
            at, here = scal[PIECE + i], scal[IS_HERE + i]

            @pl.when(here == 1)
            def _():
                upper[pl.ds(i * 64, 64), :] = up_here[at]

            @pl.when(here == 0)
            def _():
                upper[pl.ds(i * 64, 64), :] = up_core[at]

    for kk in range(KR):
        rows = pl.ds(kk * TILE, TILE)
        left = jnp.concatenate([piece[rows, :] for piece in lower], axis=1)
        acc = jnp.dot(left, upper[...], preferred_element_type=jnp.float32)
        out[rows, :] = jnp.where(listed[block * KR + kk] > 0.5, -acc, 0.0)

    def add(group):
        for spot, unit in zip(spots, group):
            start = pl.multiple_of(scal[SLOT + spot] * TILE, TILE)
            add_unit(scal, spot, block, unit, out, start)

    @pl.when(same)
    def _():
        add(units[: len(spots)])

    @pl.when(jnp.logical_not(same))
    def _():
        add(units[len(spots) :])


def base(scal, listed, lower, up_here, up_core, spots, own, other):
    n = len(spots)
    whole = pl.BlockSpec((8, 64, PC * TILE), lambda b, s: (0, 0, 0), pipeline_mode=pl.Buffered(1))
    spec = pltpu.PrefetchScalarGridSpec(
        num_scalar_prefetch=1,
        grid=(PRB // KR,),
        in_specs=[pl.BlockSpec((PRB, 1, PC * TILE), lambda b, s: (0, 0, 0))]
        + [pl.BlockSpec((HEIGHT, TILE), lambda b, s: (b, 0))] * 8
        + [whole, whole]
        + [pl.BlockSpec(UNIT, own_map)] * n
        + [pl.BlockSpec(UNIT, other_map)] * n,
        out_specs=pl.BlockSpec((HEIGHT, PC * TILE), lambda b, s: (b, 0)),
        scratch_shapes=[pltpu.VMEM((1024, PC * TILE), jnp.bfloat16)],
    )

    def kernel(*refs):
        base_kernel(spots, *refs)

    return pl.pallas_call(
        kernel,
        grid_spec=spec,
        out_shape=jax.ShapeDtypeStruct((PRB * TILE, PC * TILE), jnp.float32),
        compiler_params=pltpu.CompilerParams(vmem_limit_bytes=56 << 20),
        cost_estimate=pl.CostEstimate(
            flops=2 * 2560 * 1280 * 1024, bytes_accessed=34 << 20, transcendentals=0
        ),
        name="base",
    )(scal, listed, *lower, up_here, up_core, *own, *other)


def turn_kernel(a, b, out):
    out[...] = jnp.concatenate([a[...], b[...]], axis=0).T


def turn(a, b):
    return pl.pallas_call(
        turn_kernel,
        grid=(2,),
        in_specs=[pl.BlockSpec((64, 1280), lambda i: (0, i))] * 2,
        out_specs=pl.BlockSpec((1280, TILE), lambda i: (i, 0)),
        out_shape=jax.ShapeDtypeStruct((PRB * TILE, TILE), jnp.bfloat16),
        cost_estimate=pl.CostEstimate(flops=0, bytes_accessed=1310720, transcendentals=0),
        name="turn",
    )(a, b)


def hop(array, row_mask=0, col_mask=0):
    route = [
        (p * COLS + q, (p ^ row_mask) * COLS + (q ^ col_mask))
        for p in range(ROWS)
        for q in range(COLS)
    ]
    return lax.ppermute(array, ("row", "col"), route)


def compute(children, row_maps, col_maps, pairs, lower_panel, upper_panel):
    row = lax.axis_index("row")
    col = lax.axis_index("col")
    chip, core = row >> 1, row & 1
    rounds = column_plan()
    source_of = [[0] * COLS for _ in range(ROUNDS)]
    tile_of = np.zeros((ROUNDS, COLS), np.int32)
    slot_of = np.zeros((ROUNDS, COLS), np.int32)
    for r, owner in enumerate(rounds):
        for target, j in owner.items():
            source_of[r][target] = j // KC
            tile_of[r, j // KC] = j % KC
            slot_of[r, target] = j // 8

    low = lower_panel.T
    low_a = turn(low, hop(low, col_mask=1))
    low_b = hop(low_a, col_mask=3)
    low_1a = hop(low_a, col_mask=4)
    low_3a = hop(low_a, col_mask=12)
    low_1b = hop(low_b, col_mask=4)
    low_3b = hop(low_b, col_mask=12)
    low_2a = hop(low_1a, col_mask=12)
    low_2b = hop(low_3b, col_mask=4)
    lower = [low_a, low_b, low_1a, low_1b, low_3a, low_3b, low_2a, low_2b]
    shard = col ^ jnp.asarray(
        [4 * y + z for y in (0, 1, 3, 2) for z in (0, 1, 3, 2)], jnp.int32
    )

    up01 = jnp.concatenate([upper_panel, hop(upper_panel, row_mask=2)])
    up_here = jnp.concatenate([up01, hop(up01, row_mask=6)])
    up_core = hop(up_here, row_mask=1)
    away = row ^ (shard >> 1)
    far = away >> 1
    place = jnp.where(far >= 2, 5 - far, far)
    piece = place * 2 + (shard & 1)
    is_here = 1 - (away & 1)

    packed = pack(children, jnp.asarray(tile_of)[:, col])

    def to_chip(array):
        groups = [[2 * x + c for x in range(XS)] for c in range(2)]
        return lax.all_to_all(array, "row", 0, 0, axis_index_groups=groups, tiled=True)

    def to_holder(array, r):
        return lax.ppermute(array, "col", [(source_of[r][q], q) for q in range(COLS)])

    first = to_holder(packed[0], 0)
    held = [to_chip(first)]
    swapped = [to_chip(hop(first, col_mask=1))]
    for r in range(1, ROUNDS):
        held.append(to_holder(to_chip(packed[r]), r))
        swapped.append(hop(held[r], col_mask=1))
    core_held = [hop(array, row_mask=1) for array in held]
    core_swapped = [hop(array, row_mask=1) for array in swapped]

    slots = jnp.arange(PRB, dtype=jnp.int32)
    row_on = lax.dynamic_slice_in_dim(row_maps.reshape(2, PRB, XS), chip, 1, 2)[:, :, 0]
    row_on = (row_on == row * PRB + slots).astype(jnp.int32)
    spots = jnp.arange(PC, dtype=jnp.int32)
    col_on = lax.dynamic_slice_in_dim(col_maps.reshape(2, PC, 8), col >> 1, 1, 2)[:, :, 0]
    col_on = (col_on == col * PC + spots).astype(jnp.int32)
    slot = jnp.concatenate([jnp.asarray(slot_of)[:, col], jnp.asarray(slot_of)[:, col ^ 1]])
    by_slot = jnp.sum(
        jnp.where(slot[:, None] == spots[None, :], 1, 0)[:, None, :] * col_on[None], axis=2
    )
    scal = jnp.concatenate(
        [
            core[None],
            slot,
            by_slot.reshape(-1),
            row_on.reshape(-1),
            piece,
            is_here,
        ]
    ).astype(jnp.int32)

    row_hit = (pairs[:, 0][:, None] == row * PRB + slots[None, :]).astype(jnp.bfloat16)
    col_hit = (pairs[:, 1][:, None] == col * PC + spots[None, :]).astype(jnp.bfloat16)
    listed = jnp.dot(row_hit.T, col_hit, preferred_element_type=jnp.float32)
    listed = jnp.repeat(listed, TILE, axis=1).reshape(PRB, 1, PC * TILE)

    def units(arrays):
        return [array.reshape(UNIT[0], 2, KR, TILE, TILE) for array in arrays]

    return base(
        scal,
        listed,
        lower,
        up_here.reshape(8, 64, PC * TILE),
        up_core.reshape(8, 64, PC * TILE),
        list(range(2 * ROUNDS)),
        units(held + swapped),
        units(core_held + core_swapped),
    )


def solution(mesh):
    placed = (P("row", "col"), P(), P(), P(), P("row", "col"), P("row", "col"))
    return jax.shard_map(
        compute, mesh=mesh, in_specs=placed, out_specs=P("row", "col"), check_vma=False
    )
```
